32 devices in a mesh: domain: 8 (over z, y), vec: 4 (over x, core).
Axes of the slice: x: 2, y: 2, z: 4, core: 2. Of those that a mesh axis runs over, the one named last changes fastest.
Arguments:
- vectors: float32 [4096, 512], P('domain', 'vec'), may hold values from -6 to 6
- hamiltonian: float32 [512, 128, 128], P('domain'), may hold values from -0.09375 to 0.09375
- tile_pairs: int32 [512, 2], P('domain'), may hold values from 0 to 31, as said below
- tile_counts: int32 [8], P('domain'), may hold values from 8 to 64, as said below
Outputs:
- filtered: float32 [4096, 512], P('domain', 'vec')
- gram: float32 [512, 512], P('vec')
The draws below stay inside these ranges and needn't reach their ends.
Inputs may be any that keep to these rules, and one draw needn't show every extreme that they name: `tile_pairs`: slots k * 64 to (k + 1) * 64 - 1 have their row group r among groups k * 4 to (k + 1) * 4 - 1 and their column group c with r <= c <= min(k * 4 + 3 * 4 - 1, 31); pairs may repeat, and repeated blocks add. `tile_counts`: one domain index uses all 64 slots.
All inputs are finite; a program needn't handle non-finite values.
Results may differ from the reference program's by a relative error of at most 0.0003.
Values sent between devices are 32-bit elements; how exact they have to be, the bound alone decides.
A program may use at most 64 MiB of HBM per device.

```python
import jax
import jax.numpy as jnp
from jax import lax

TILE = 128
COLS = 512
G_DEV = 4
TILE_DEV = 64
REACH = 2
NGROUPS = 32
SLOTS = 512
ROWS = 4096


def draw_tile_pairs(key, part):
    ndev = NGROUPS // G_DEV
    first_key, second_key = jax.random.split(jax.random.fold_in(key, 11))
    span = (REACH + 1) * G_DEV
    row_loc = jax.random.randint(first_key, (ndev, TILE_DEV), 0, G_DEV)
    offset = jax.random.randint(second_key, (ndev, TILE_DEV), 0, span)
    col_loc = row_loc + offset % (span - row_loc)
    slot = jnp.arange(TILE_DEV, dtype=jnp.int32)[None, :]
    row_loc = jnp.where(slot == 0, 0, row_loc)
    col_loc = jnp.where(slot == 0, span - 1, col_loc)
    base = jnp.arange(ndev, dtype=jnp.int32)[:, None] * G_DEV
    row_grp = base + row_loc
    col_grp = jnp.minimum(base + col_loc, NGROUPS - 1)
    return jnp.stack([row_grp, col_grp], -1).reshape(SLOTS, 2).astype(jnp.int32)


def draw_tile_counts(key, part):
    ndev = NGROUPS // G_DEV
    first_key, second_key = jax.random.split(jax.random.fold_in(key, 23))
    counts = jax.random.randint(first_key, (ndev,), TILE_DEV // 8, TILE_DEV // 2 + 1)
    busiest = jax.random.randint(second_key, (), 0, ndev)
    counts = jnp.where(jnp.arange(ndev, dtype=jnp.int32) == busiest, TILE_DEV, counts)
    return counts.astype(jnp.int32)


def levels(rng, dims, shards, least, top_value):
    loudness = 1.0
    for position, parts in shards:
        draws = jax.random.uniform(jax.random.fold_in(jax.random.fold_in(rng, 6), position), (parts,), jnp.float32, least / len(shards), top_value / len(shards))
        loudness = loudness * jnp.repeat(jnp.exp(draws), dims[position] // parts).reshape((-1,) + (1,) * (len(dims) - 1 - position))
    return loudness


def centred(own_key, dims, scale, reach, shards=(), kind=jnp.bfloat16):
    loudness = levels(own_key, dims, shards, -0.22, 0.18) if shards else 1.0
    values = jax.random.normal(own_key, dims, jnp.float32) * scale * loudness
    return jnp.minimum(jnp.maximum(values, -reach), reach).astype(kind)


def setup_inputs(seed: int = 0) -> dict:
    keys = jax.random.split(jax.random.key(seed), 5)
    return {
        "vectors": centred(keys[0], (ROWS, COLS), 1.0, 6.0, ((0, 8), (1, 4)), jnp.float32),
        "hamiltonian": centred(keys[1], (SLOTS, TILE, TILE), (2 * TILE * TILE_DEV // G_DEV) ** -0.5, 0.09375, ((0, 8),), jnp.float32),
        "tile_pairs": draw_tile_pairs(jax.random.fold_in(keys[4], 71), 0),
        "tile_counts": draw_tile_counts(jax.random.fold_in(keys[4], 71), 0),
    }


center_shift = 1.0
half_width = 1.5


def apply_ham(block, hamiltonian, tile_pairs, weights):
    grouped = block.reshape(NGROUPS, TILE, COLS)
    total_slots = hamiltonian.shape[0]
    tiles = hamiltonian.reshape(total_slots // 64, 64, TILE, TILE)
    rows = tile_pairs[:, 0].reshape(total_slots // 64, 64)
    cols = tile_pairs[:, 1].reshape(total_slots // 64, 64)
    wts = weights.reshape(total_slots // 64, 64)

    def one_block(acc, items):
        tile, row_ids, col_ids, wgt = items
        diag = row_ids == col_ids
        tile = jnp.where(diag[:, None, None], 0.5 * (tile + jnp.swapaxes(tile, 1, 2)), tile)
        fwd = jnp.einsum("tij,tjc->tic", tile, grouped[col_ids], precision=lax.Precision.HIGHEST)
        back = jnp.einsum("tji,tjc->tic", tile, grouped[row_ids], precision=lax.Precision.HIGHEST)
        fwd = fwd * wgt[:, None, None]
        back = back * (wgt * (1.0 - diag.astype(jnp.float32)))[:, None, None]
        acc = acc.at[row_ids].add(fwd)
        acc = acc.at[col_ids].add(back)
        return acc, None

    start = jnp.zeros((NGROUPS, TILE, COLS), jnp.float32)
    result, _ = lax.scan(one_block, start, (tiles, rows, cols, wts))
    return result.reshape(NGROUPS * TILE, COLS)


def reference(vectors, hamiltonian, tile_pairs, tile_counts):
    total_slots = hamiltonian.shape[0]
    slot_ids = jnp.arange(total_slots, dtype=jnp.int32)
    owners = slot_ids // TILE_DEV
    weights = (slot_ids % TILE_DEV < tile_counts[owners]).astype(jnp.float32)
    first = vectors
    second = (apply_ham(first, hamiltonian, tile_pairs, weights) - center_shift * first) / half_width
    third = 2.0 * (apply_ham(second, hamiltonian, tile_pairs, weights) - center_shift * second) / half_width - first
    filtered = 2.0 * (apply_ham(third, hamiltonian, tile_pairs, weights) - center_shift * third) / half_width - second
    gram = jnp.dot(filtered.T, filtered, precision=lax.Precision.HIGHEST, preferred_element_type=jnp.float32) / ROWS
    return filtered, gram
```

```python
import functools

import jax
import jax.numpy as jnp
from jax import lax
from jax.experimental import pallas as pl
from jax.experimental.pallas import tpu as pltpu
from jax.sharding import PartitionSpec as P

TILE = 128
REACH = 2
CHUNK = 8

center_shift = 1.0
half_width = 1.5

F32 = jnp.float32
BF16 = jnp.bfloat16


def densify_kernel(groups, pairs_ref, count_ref, ham_ref, dense_ref, tiles, sems):
    slots = ham_ref.shape[0]
    chunk = CHUNK if slots % CHUNK == 0 else slots
    count = count_ref[0]
    base = lax.axis_index("domain") * groups

    def copy(index):
        part = pl.ds(index * chunk, chunk)
        return pltpu.make_async_copy(ham_ref.at[part], tiles.at[part], sems.at[index])

    for index in range(slots // chunk):

        @pl.when(count > index * chunk)
        def _():
            copy(index).start()

    dense_ref[...] = jnp.zeros_like(dense_ref)

    def add(slot, carry):
        row = pairs_ref[slot, 0]
        col = pairs_ref[slot, 1]
        scale = jnp.where(row == col, 0.5, 1.0).astype(F32)
        rows = pl.ds(pl.multiple_of((row - base) * TILE, TILE), TILE)
        cols = pl.ds(pl.multiple_of((col - base) * TILE, TILE), TILE)
        dense_ref[rows, cols] += tiles[slot] * scale
        return carry

    for index in range(slots // chunk):

        @pl.when(count > index * chunk)
        def _():
            copy(index).wait()
            lax.fori_loop(index * chunk, jnp.minimum(count, (index + 1) * chunk), add, 0)


def densify(hamiltonian, tile_pairs, tile_counts, groups):
    slots = hamiltonian.shape[0]
    return pl.pallas_call(
        functools.partial(densify_kernel, groups),
        out_shape=jax.ShapeDtypeStruct((groups * TILE, (REACH + 1) * groups * TILE), F32),
        in_specs=[
            pl.BlockSpec(memory_space=pltpu.SMEM),
            pl.BlockSpec(memory_space=pltpu.SMEM),
            pl.BlockSpec(memory_space=pl.ANY),
        ],
        out_specs=pl.BlockSpec(memory_space=pltpu.VMEM),
        scratch_shapes=[
            pltpu.VMEM(hamiltonian.shape, F32),
            pltpu.SemaphoreType.DMA((slots // CHUNK + 1,)),
        ],
        name="densify",
    )(tile_pairs, tile_counts, hamiltonian)


def halves(value):
    high = value.astype(BF16)
    low = (value - high.astype(F32)).astype(BF16)
    return high, low


def stacked(value):
    return jnp.concatenate(halves(value), 1)


def product(high, low, both):
    wide = jnp.dot(high, both, preferred_element_type=F32)
    wide = wide + jnp.dot(low, both, preferred_element_type=F32)
    width = both.shape[1] // 2
    return wide[:, :width] + wide[:, width:]


def filter_kernel(n, m, with_gram, x_ref, dense_hbm, *refs):
    if with_gram:
        f_ref, g_ref, *refs = refs
    else:
        f_ref, *refs = refs
    (dense, fwd_h, fwd_l, back_h, back_l, both, acc, x1_ref, x2_ref, in_x, in_b, out_b) = refs[:12]
    (load_sem, xs_sem, xr_sem, bs_sem, br_sem) = refs[12:17]
    me = lax.axis_index("domain")
    mine = lax.axis_index("vec")
    rows, width = x_ref.shape

    load = pltpu.make_async_copy(dense_hbm, dense, load_sem)
    load.start()

    barrier = pltpu.get_barrier_semaphore()
    if with_gram:
        for d in range(1, n):
            pl.semaphore_signal(barrier, inc=1, device_id={"domain": (me + d) % n})
        for d in range(1, m):
            pl.semaphore_signal(barrier, inc=1, device_id={"vec": (mine + d) % m})
        pl.semaphore_wait(barrier, n - 1 + m - 1)
    else:
        for d in range(1, REACH + 1):

            @pl.when(me >= d)
            def _():
                pl.semaphore_signal(barrier, inc=1, device_id={"domain": me - d})

            @pl.when(me + d < n)
            def _():
                pl.semaphore_signal(barrier, inc=1, device_id={"domain": me + d})

        for d in range(1, REACH + 1):

            @pl.when(me >= d)
            def _():
                pl.semaphore_wait(barrier, 1)

            @pl.when(me + d < n)
            def _():
                pl.semaphore_wait(barrier, 1)

    def x_copy(step, d, source):
        return pltpu.make_async_remote_copy(
            src_ref=source,
            dst_ref=in_x.at[step, d - 1],
            send_sem=xs_sem.at[step, d - 1],
            recv_sem=xr_sem.at[step, d - 1],
            device_id={"domain": me - d},
        )

    def b_copy(step, d):
        return pltpu.make_async_remote_copy(
            src_ref=out_b.at[step, d - 1],
            dst_ref=in_b.at[step, d - 1],
            send_sem=bs_sem.at[step, d - 1],
            recv_sem=br_sem.at[step, d - 1],
            device_id={"domain": me + d},
        )

    sources = (x_ref, x1_ref, x2_ref)
    for step in range(3):
        source = sources[step]
        for d in range(1, REACH + 1):

            @pl.when(me >= d)
            def _():
                x_copy(step, d, source).start()

        both[...] = stacked(source[...])
        if step == 0:
            load.wait()
        for d in range(1, REACH + 1):

            @pl.when(me + d < n)
            def _():
                if step == 0:
                    block = dense[:, d * rows : (d + 1) * rows]
                    back_h[d - 1], back_l[d - 1] = halves(block.T)
                out_b[step, d - 1] = product(back_h[d - 1], back_l[d - 1], both[...])
                b_copy(step, d).start()

        if step == 0:
            block = dense[:, :rows]
            fwd_h[0], fwd_l[0] = halves(block + block.T)
            for d in range(1, REACH + 1):
                fwd_h[d], fwd_l[d] = halves(dense[:, d * rows : (d + 1) * rows])
        acc[...] = product(fwd_h[0], fwd_l[0], both[...])
        for d in range(1, REACH + 1):

            @pl.when(me + d < n)
            def _():
                x_copy(step, d, source).wait_recv()
                acc[...] += product(fwd_h[d], fwd_l[d], stacked(in_x[step, d - 1]))

        for d in range(1, REACH + 1):

            @pl.when(me >= d)
            def _():
                b_copy(step, d).wait_recv()
                acc[...] += in_b[step, d - 1]

        if step == 0:
            x1_ref[...] = (acc[...] - center_shift * x_ref[...]) / half_width
        elif step == 1:
            x2_ref[...] = 2.0 * (acc[...] - center_shift * x1_ref[...]) / half_width - x_ref[...]
        else:
            f_ref[...] = 2.0 * (acc[...] - center_shift * x2_ref[...]) / half_width - x1_ref[...]

    if with_gram:
        (in_f, part, in_g, g_mine) = refs[17:21]
        (fs_sem, fr_sem, gs_sem, gr_sem, hs_sem, hr_sem) = refs[21:]
        far = (mine + 2) % 4
        near = mine + 1 - 2 * (mine % 2)
        cross = (near + 2) % 4

        def f_copy(index, source, target):
            return pltpu.make_async_remote_copy(
                src_ref=source,
                dst_ref=in_f.at[index],
                send_sem=fs_sem.at[index],
                recv_sem=fr_sem.at[index],
                device_id={"vec": target},
            )

        to_far = f_copy(0, f_ref, far)
        to_near = f_copy(1, f_ref, near)
        relay = f_copy(2, in_f.at[0], near)
        to_far.start()
        to_near.start()
        left_h, left_l = halves(f_ref[...].T)
        back_h[0, :width], back_l[0, :width] = left_h, left_l
        total = rows * n

        def gram_block(value, owner):
            block = product(back_h[0, :width], back_l[0, :width], stacked(value)) / total
            part[:, pl.ds(pl.multiple_of(owner * width, width), width)] = block

        gram_block(f_ref[...], mine)
        to_near.wait_recv()
        gram_block(in_f[1], near)
        to_far.wait_recv()
        relay.start()
        gram_block(in_f[0], far)
        relay.wait_recv()
        gram_block(in_f[2], cross)

        piece = width // n

        def rows_of(owner):
            return pl.ds(pl.multiple_of(owner * piece, piece), piece)

        def g_copy(d):
            peer = (me + d) % n
            return pltpu.make_async_remote_copy(
                src_ref=part.at[rows_of(peer)],
                dst_ref=in_g.at[d],
                send_sem=gs_sem.at[d],
                recv_sem=gr_sem.at[d],
                device_id={"domain": peer},
            )

        def h_copy(d, owner):
            return pltpu.make_async_remote_copy(
                src_ref=g_mine,
                dst_ref=g_ref.at[rows_of(owner)],
                send_sem=hs_sem.at[d],
                recv_sem=hr_sem.at[d],
                device_id={"domain": (me + d) % n},
            )

        for d in range(1, n):
            g_copy(d).start()
        block = part[rows_of(me)]
        for d in range(1, n):
            g_copy(d).wait_recv()
            block = block + in_g[d]
        g_mine[...] = block
        for d in range(1, n):
            h_copy(d, me).start()
        g_ref[rows_of(me)] = block
        for d in range(1, n):
            h_copy(d, (me + n - d) % n).wait_recv()
        to_far.wait_send()
        to_near.wait_send()
        relay.wait_send()
        for d in range(1, n):
            g_copy(d).wait_send()
            h_copy(d, me).wait_send()

    for step in range(3):
        for d in range(1, REACH + 1):

            @pl.when(me >= d)
            def _():
                x_copy(step, d, sources[step]).wait_send()

            @pl.when(me + d < n)
            def _():
                b_copy(step, d).wait_send()


def shards(vectors, hamiltonian, tile_pairs, tile_counts):
    n = lax.axis_size("domain")
    m = lax.axis_size("vec")
    rows, width = vectors.shape
    groups = rows // TILE
    dense = densify(hamiltonian, tile_pairs, tile_counts, groups)
    with_gram = m == 4 and width % (8 * n) == 0
    dma = pltpu.SemaphoreType.DMA
    out_shape = [jax.ShapeDtypeStruct((rows, width), F32)]
    scratch = [
        pltpu.VMEM(dense.shape, F32),
        pltpu.VMEM((REACH + 1, rows, rows), BF16),
        pltpu.VMEM((REACH + 1, rows, rows), BF16),
        pltpu.VMEM((REACH, rows, rows), BF16),
        pltpu.VMEM((REACH, rows, rows), BF16),
        pltpu.VMEM((rows, 2 * width), BF16),
        pltpu.VMEM((rows, width), F32),
        pltpu.VMEM((rows, width), F32),
        pltpu.VMEM((rows, width), F32),
        pltpu.VMEM((3, REACH, rows, width), F32),
        pltpu.VMEM((3, REACH, rows, width), F32),
        pltpu.VMEM((3, REACH, rows, width), F32),
        dma,
        dma((3, REACH)),
        dma((3, REACH)),
        dma((3, REACH)),
        dma((3, REACH)),
    ]
    if with_gram:
        out_shape.append(jax.ShapeDtypeStruct((width, m * width), F32))
        scratch += [
            pltpu.VMEM((3, rows, width), F32),
            pltpu.VMEM((width, m * width), F32),
            pltpu.VMEM((n, width // n, m * width), F32),
            pltpu.VMEM((width // n, m * width), F32),
            dma((3,)),
            dma((3,)),
            dma((n,)),
            dma((n,)),
            dma((n,)),
            dma((n,)),
        ]
    outs = pl.pallas_call(
        functools.partial(filter_kernel, n, m, with_gram),
        out_shape=out_shape,
        in_specs=[pl.BlockSpec(memory_space=pltpu.VMEM), pl.BlockSpec(memory_space=pl.ANY)],
        out_specs=[pl.BlockSpec(memory_space=pltpu.VMEM)] * len(out_shape),
        scratch_shapes=scratch,
        compiler_params=pltpu.CompilerParams(
            collective_id=0, has_side_effects=True, vmem_limit_bytes=50 * 2**20
        ),
        name="chebyshev",
    )(vectors, dense)
    if with_gram:
        return tuple(outs)
    (filtered,) = outs
    gathered = lax.all_gather(filtered, "vec", axis=1, tiled=True)
    partial_block = jnp.dot(
        filtered.T, gathered, precision=lax.Precision.HIGHEST, preferred_element_type=F32
    ) / (rows * n)
    return (filtered, lax.psum(partial_block, "domain"))


def solution(mesh):
    in_specs = (P("domain", "vec"), P("domain", None, None), P("domain", None), P("domain"))
    out_specs = (P("domain", "vec"), P("vec", None))
    return jax.shard_map(shards, mesh=mesh, in_specs=in_specs, out_specs=out_specs, check_vma=False)
```

```python
import functools

import jax
import jax.numpy as jnp
from jax import lax
from jax.experimental import pallas as pl
from jax.experimental.pallas import tpu as pltpu
from jax.sharding import PartitionSpec as P

TILE = 128
REACH = 2

center_shift = 1.0
half_width = 1.5

F32 = jnp.float32
BF16 = jnp.bfloat16


def index_kernel(groups, span, pairs_ref, count_ref, before_ref, last_ref):
    slots = pairs_ref.shape[1]
    count = count_ref[0]
    base = lax.axis_index("domain") * groups

    def clear(block, carry):
        last_ref[block] = -1
        return carry

    def chain(slot, carry):
        block = (pairs_ref[0, slot] - base) * span + pairs_ref[1, slot] - base
        before_ref[slot] = last_ref[block]
        last_ref[block] = slot
        return carry

    def skip(slot, carry):
        before_ref[slot] = -1
        return carry

    lax.fori_loop(0, groups * span, clear, 0)
    lax.fori_loop(0, count, chain, 0)
    lax.fori_loop(count, slots, skip, 0)


def index_slots(tile_pairs, tile_counts, groups):
    span = (REACH + 1) * groups
    smem = pl.BlockSpec(memory_space=pltpu.SMEM)
    return pl.pallas_call(
        functools.partial(index_kernel, groups, span),
        out_shape=[
            jax.ShapeDtypeStruct((tile_pairs.shape[0],), jnp.int32),
            jax.ShapeDtypeStruct((groups * span,), jnp.int32),
        ],
        in_specs=[smem, smem],
        out_specs=[smem, smem],
        name="index_slots",
    )(tile_pairs.T, tile_counts)


def halves(value):
    high = value.astype(BF16)
    low = (value - high.astype(F32)).astype(BF16)
    return high, low


def stacked(value):
    return jnp.concatenate(halves(value), 1)


def product(high, low, both):
    wide = jnp.dot(high, both, preferred_element_type=F32)
    wide = wide + jnp.dot(low, both, preferred_element_type=F32)
    width = both.shape[1] // 2
    return wide[:, :width] + wide[:, width:]


def filter_kernel(n, m, with_gram, x_ref, before_ref, last_ref, ham_ref, *refs):
    if with_gram:
        f_ref, g_ref, *refs = refs
    else:
        f_ref, *refs = refs
    (tiles, fwd_h, fwd_l, back_h, back_l, both, acc, x1_ref, x2_ref, in_x, in_b, out_b) = refs[:12]
    (load_sem, xs_sem, xr_sem, bs_sem, br_sem) = refs[12:17]
    me = lax.axis_index("domain")
    mine = lax.axis_index("vec")
    rows, width = x_ref.shape
    groups = rows // TILE
    span = (REACH + 1) * groups

    load = pltpu.make_async_copy(ham_ref, tiles, load_sem)
    load.start()

    barrier = pltpu.get_barrier_semaphore()
    if with_gram:
        for d in range(1, n):
            pl.semaphore_signal(barrier, inc=1, device_id={"domain": (me + d) % n})
        for d in range(1, m):
            pl.semaphore_signal(barrier, inc=1, device_id={"vec": (mine + d) % m})
        pl.semaphore_wait(barrier, n - 1 + m - 1)
    else:
        for d in range(1, REACH + 1):

            @pl.when(me >= d)
            def _():
                pl.semaphore_signal(barrier, inc=1, device_id={"domain": me - d})

            @pl.when(me + d < n)
            def _():
                pl.semaphore_signal(barrier, inc=1, device_id={"domain": me + d})

        for d in range(1, REACH + 1):

            @pl.when(me >= d)
            def _():
                pl.semaphore_wait(barrier, 1)

            @pl.when(me + d < n)
            def _():
                pl.semaphore_wait(barrier, 1)

    def rows_at(group):
        return pl.ds(group * TILE, TILE)

    sources = (x_ref, x1_ref, x2_ref)

    def x_copy(step, d, group):
        return pltpu.make_async_remote_copy(
            src_ref=sources[step].at[rows_at(group)],
            dst_ref=in_x.at[step, d - 1, rows_at(group)],
            send_sem=xs_sem.at[step, d - 1, group],
            recv_sem=xr_sem.at[step, d - 1, group],
            device_id={"domain": me - d},
        )

    def b_copy(step, d, group):
        return pltpu.make_async_remote_copy(
            src_ref=out_b.at[step, d - 1, rows_at(group)],
            dst_ref=in_b.at[step, d - 1, rows_at(group)],
            send_sem=bs_sem.at[step, d - 1, group],
            recv_sem=br_sem.at[step, d - 1, group],
            device_id={"domain": me + d},
        )

    def send_x(step, group):
        for d in range(1, REACH + 1):

            @pl.when(me >= d)
            def _():
                x_copy(step, d, group).start()

    if with_gram:
        (in_f, part, in_g1, out_g, in_g2, g_mine) = refs[17:23]
        (fs_sem, fr_sem, g1s_sem, g1r_sem, g2s_sem, g2r_sem, hs_sem, hr_sem, ks_sem, kr_sem) = refs[23:]
        far = (mine + 2) % 4
        near = mine + 1 - 2 * (mine % 2)
        cross = (near + 2) % 4

        def f_copy(index, group):
            source = in_f.at[0] if index == 2 else f_ref
            return pltpu.make_async_remote_copy(
                src_ref=source.at[rows_at(group)],
                dst_ref=in_f.at[index, rows_at(group)],
                send_sem=fs_sem.at[index, group],
                recv_sem=fr_sem.at[index, group],
                device_id={"vec": far if index == 0 else near},
            )

    for group in range(groups):
        send_x(0, group)

    both[...] = stacked(x_ref[...])
    load.wait()

    def add_before(slot, carry):
        before = before_ref[slot]
        weight = (before >= 0).astype(F32)
        tiles[slot] = tiles[slot] + tiles[jnp.maximum(before, 0)] * weight
        return carry

    lax.fori_loop(0, tiles.shape[0], add_before, 0)

    def block_at(row, col):
        slot = last_ref[row * span + col]
        return tiles[jnp.maximum(slot, 0)] * (slot >= 0).astype(F32)

    def put(high, low, index, row, col, value):
        high[index, rows_at(row), rows_at(col)], low[index, rows_at(row), rows_at(col)] = halves(value)

    for d in range(1, REACH + 1):
        for row in range(groups):
            for col in range(groups):
                block = block_at(row, d * groups + col)
                put(fwd_h, fwd_l, d, row, col, block)
                put(back_h, back_l, d - 1, col, row, block.T)
    for row in range(groups):
        for col in range(row, groups):
            block = block_at(row, col)
            if row == col:
                put(fwd_h, fwd_l, 0, row, col, 0.5 * (block + block.T))
            else:
                put(fwd_h, fwd_l, 0, row, col, block)
                put(fwd_h, fwd_l, 0, col, row, block.T)

    for step in range(3):
        if step > 0:
            both[...] = stacked(sources[step][...])
        for d in range(1, REACH + 1):

            @pl.when(me + d < n)
            def _():
                out_b[step, d - 1] = product(back_h[d - 1], back_l[d - 1], both[...])

        for group in range(groups):
            for d in range(1, REACH + 1):

                @pl.when(me + d < n)
                def _():
                    b_copy(step, d, group).start()

        acc[...] = product(fwd_h[0], fwd_l[0], both[...])
        for d in range(1, REACH + 1):

            @pl.when(me + d < n)
            def _():
                for group in range(groups):
                    x_copy(step, d, group).wait_recv()
                acc[...] += product(fwd_h[d], fwd_l[d], stacked(in_x[step, d - 1]))

        for group in range(groups):
            here = rows_at(group)
            for d in range(1, REACH + 1):

                @pl.when(me >= d)
                def _():
                    b_copy(step, d, group).wait_recv()
                    acc[here] += in_b[step, d - 1, here]

            if step == 0:
                x1_ref[here] = (acc[here] - center_shift * x_ref[here]) / half_width
            elif step == 1:
                x2_ref[here] = 2.0 * (acc[here] - center_shift * x1_ref[here]) / half_width - x_ref[here]
            else:
                f_ref[here] = 2.0 * (acc[here] - center_shift * x2_ref[here]) / half_width - x1_ref[here]
            if step < 2:
                send_x(step + 1, group)
            elif with_gram:
                f_copy(0, group).start()
                f_copy(1, group).start()

    if with_gram:
        left_h, left_l = halves(f_ref[...].T)
        back_h[0, :width], back_l[0, :width] = left_h, left_l
        total = rows * n

        def gram_block(value, owner):
            block = product(back_h[0, :width], back_l[0, :width], stacked(value)) / total
            part[:, pl.ds(pl.multiple_of(owner * width, width), width)] = block

        for group in range(groups):
            f_copy(0, group).wait_recv()
            f_copy(2, group).start()
        gram_block(f_ref[...], mine)
        for group in range(groups):
            f_copy(1, group).wait_recv()
        gram_block(in_f[1], near)
        gram_block(in_f[0], far)
        for group in range(groups):
            f_copy(2, group).wait_recv()
        gram_block(in_f[2], cross)

        piece = width // n
        pairs = n // 2
        pair = me // 2
        side = me % 2
        mate = me + 1 - 2 * side

        def rows_of(owner):
            return pl.ds(pl.multiple_of(owner * piece, piece), piece)

        def g1_copy(d):
            return pltpu.make_async_remote_copy(
                src_ref=part.at[rows_of(2 * ((pair + d) % pairs) + 1 - side)],
                dst_ref=in_g1.at[d],
                send_sem=g1s_sem.at[d],
                recv_sem=g1r_sem.at[d],
                device_id={"domain": mate},
            )

        def g2_copy(d):
            return pltpu.make_async_remote_copy(
                src_ref=out_g.at[d],
                dst_ref=in_g2.at[d],
                send_sem=g2s_sem.at[d],
                recv_sem=g2r_sem.at[d],
                device_id={"domain": 2 * ((pair + d) % pairs) + side},
            )

        def h_copy(d):
            return pltpu.make_async_remote_copy(
                src_ref=g_mine,
                dst_ref=g_ref.at[rows_of(me)],
                send_sem=hs_sem.at[d],
                recv_sem=hr_sem.at[d],
                device_id={"domain": 2 * ((pair + d) % pairs) + side},
            )

        def k_copy(d):
            owned = rows_of(2 * ((pair + pairs - d) % pairs) + side)
            return pltpu.make_async_remote_copy(
                src_ref=g_mine if d == 0 else g_ref.at[owned],
                dst_ref=g_ref.at[owned],
                send_sem=ks_sem.at[d],
                recv_sem=kr_sem.at[d],
                device_id={"domain": mate},
            )

        order = list(range(1, pairs)) + [0]
        for d in order:
            g1_copy(d).start()
        for d in order:
            g1_copy(d).wait_recv()
            block = part[rows_of(2 * ((pair + d) % pairs) + side)] + in_g1[d]
            if d > 0:
                out_g[d] = block
                g2_copy(d).start()
        for d in range(1, pairs):
            g2_copy(d).wait_recv()
            block = block + in_g2[d]
        g_mine[...] = block
        for d in range(1, pairs):
            h_copy(d).start()
        k_copy(0).start()
        g_ref[rows_of(me)] = block
        for d in range(1, pairs):
            h_copy(d).wait_recv()
            k_copy(d).start()
        for d in range(pairs):
            k_copy(d).wait_recv()
        for group in range(groups):
            for index in range(3):
                f_copy(index, group).wait_send()
        for d in range(pairs):
            g1_copy(d).wait_send()
            k_copy(d).wait_send()
        for d in range(1, pairs):
            g2_copy(d).wait_send()
            h_copy(d).wait_send()

    for step in range(3):
        for d in range(1, REACH + 1):

            @pl.when(me >= d)
            def _():
                for group in range(groups):
                    x_copy(step, d, group).wait_send()

            @pl.when(me + d < n)
            def _():
                for group in range(groups):
                    b_copy(step, d, group).wait_send()


def shards(vectors, hamiltonian, tile_pairs, tile_counts):
    n = lax.axis_size("domain")
    m = lax.axis_size("vec")
    rows, width = vectors.shape
    groups = rows // TILE
    before, last = index_slots(tile_pairs, tile_counts, groups)
    with_gram = m == 4 and n % 2 == 0 and width % (8 * n) == 0
    dma = pltpu.SemaphoreType.DMA
    out_shape = [jax.ShapeDtypeStruct((rows, width), F32)]
    scratch = [
        pltpu.VMEM(hamiltonian.shape, F32),
        pltpu.VMEM((REACH + 1, rows, rows), BF16),
        pltpu.VMEM((REACH + 1, rows, rows), BF16),
        pltpu.VMEM((REACH, rows, rows), BF16),
        pltpu.VMEM((REACH, rows, rows), BF16),
        pltpu.VMEM((rows, 2 * width), BF16),
        pltpu.VMEM((rows, width), F32),
        pltpu.VMEM((rows, width), F32),
        pltpu.VMEM((rows, width), F32),
        pltpu.VMEM((3, REACH, rows, width), F32),
        pltpu.VMEM((3, REACH, rows, width), F32),
        pltpu.VMEM((3, REACH, rows, width), F32),
        dma,
        dma((3, REACH, groups)),
        dma((3, REACH, groups)),
        dma((3, REACH, groups)),
        dma((3, REACH, groups)),
    ]
    if with_gram:
        out_shape.append(jax.ShapeDtypeStruct((width, m * width), F32))
        scratch += [
            pltpu.VMEM((3, rows, width), F32),
            pltpu.VMEM((width, m * width), F32),
            pltpu.VMEM((n // 2, width // n, m * width), F32),
            pltpu.VMEM((n // 2, width // n, m * width), F32),
            pltpu.VMEM((n // 2, width // n, m * width), F32),
            pltpu.VMEM((width // n, m * width), F32),
            dma((3, groups)),
            dma((3, groups)),
        ]
        scratch += [dma((n // 2,))] * 8
    outs = pl.pallas_call(
        functools.partial(filter_kernel, n, m, with_gram),
        out_shape=out_shape,
        in_specs=[
            pl.BlockSpec(memory_space=pltpu.VMEM),
            pl.BlockSpec(memory_space=pltpu.SMEM),
            pl.BlockSpec(memory_space=pltpu.SMEM),
            pl.BlockSpec(memory_space=pl.ANY),
        ],
        out_specs=[pl.BlockSpec(memory_space=pltpu.VMEM)] * len(out_shape),
        scratch_shapes=scratch,
        compiler_params=pltpu.CompilerParams(
            collective_id=0, has_side_effects=True, vmem_limit_bytes=62 * 2**20
        ),
        name="chebyshev",
    )(vectors, before, last, hamiltonian)
    if with_gram:
        return tuple(outs)
    (filtered,) = outs
    gathered = lax.all_gather(filtered, "vec", axis=1, tiled=True)
    partial_block = jnp.dot(
        filtered.T, gathered, precision=lax.Precision.HIGHEST, preferred_element_type=F32
    ) / (rows * n)
    return (filtered, lax.psum(partial_block, "domain"))


def solution(mesh):
    in_specs = (P("domain", "vec"), P("domain", None, None), P("domain", None), P("domain"))
    out_specs = (P("domain", "vec"), P("vec", None))
    return jax.shard_map(shards, mesh=mesh, in_specs=in_specs, out_specs=out_specs, check_vma=False)
```

```python
import functools

import jax
import jax.numpy as jnp
from jax import lax
from jax.experimental import pallas as pl
from jax.experimental.pallas import tpu as pltpu
from jax.sharding import PartitionSpec as P

TILE = 128
REACH = 2

center_shift = 1.0
half_width = 1.5

F32 = jnp.float32
BF16 = jnp.bfloat16


def index_kernel(groups, span, pairs_ref, count_ref, before_ref, last_ref):
    slots = pairs_ref.shape[1]
    count = count_ref[0]
    base = lax.axis_index("domain") * groups

    def clear(block, carry):
        last_ref[block] = -1
        return carry

    def chain(slot, carry):
        block = (pairs_ref[0, slot] - base) * span + pairs_ref[1, slot] - base
        before_ref[slot] = last_ref[block]
        last_ref[block] = slot
        return carry

    def skip(slot, carry):
        before_ref[slot] = -1
        return carry

    lax.fori_loop(0, groups * span, clear, 0)
    lax.fori_loop(0, count, chain, 0)
    lax.fori_loop(count, slots, skip, 0)


def index_slots(tile_pairs, tile_counts, groups):
    span = (REACH + 1) * groups
    smem = pl.BlockSpec(memory_space=pltpu.SMEM)
    return pl.pallas_call(
        functools.partial(index_kernel, groups, span),
        out_shape=[
            jax.ShapeDtypeStruct((tile_pairs.shape[0],), jnp.int32),
            jax.ShapeDtypeStruct((groups * span,), jnp.int32),
        ],
        in_specs=[smem, smem],
        out_specs=[smem, smem],
        name="index_slots",
    )(tile_pairs.T, tile_counts)


def halves(value):
    high = value.astype(BF16)
    low = (value - high.astype(F32)).astype(BF16)
    return high, low


def stacked(value):
    return jnp.concatenate(halves(value), 1)


def product(high, low, both):
    wide = jnp.dot(high, both, preferred_element_type=F32)
    wide = wide + jnp.dot(low, both, preferred_element_type=F32)
    width = both.shape[1] // 2
    return wide[:, :width] + wide[:, width:]


def filter_kernel(n, m, with_gram, x_ref, before_ref, last_ref, ham_ref, *refs):
    if with_gram:
        f_ref, g_ref, *refs = refs
    else:
        f_ref, *refs = refs
    (tiles, fwd_h, fwd_l, back_h, back_l, both, acc, x1_ref, x2_ref, in_x, in_b, out_b) = refs[:12]
    (load_sem, xs_sem, xr_sem, bs_sem, br_sem) = refs[12:17]
    me = lax.axis_index("domain")
    mine = lax.axis_index("vec")
    rows, width = x_ref.shape
    groups = rows // TILE
    span = (REACH + 1) * groups

    load = pltpu.make_async_copy(ham_ref, tiles, load_sem)
    load.start()

    barrier = pltpu.get_barrier_semaphore()
    if with_gram:
        for d in range(1, n):
            pl.semaphore_signal(barrier, inc=1, device_id={"domain": (me + d) % n})
        for d in range(1, m):
            pl.semaphore_signal(barrier, inc=1, device_id={"vec": (mine + d) % m})
        pl.semaphore_wait(barrier, n - 1 + m - 1)
    else:
        for d in range(1, REACH + 1):

            @pl.when(me >= d)
            def _():
                pl.semaphore_signal(barrier, inc=1, device_id={"domain": me - d})

            @pl.when(me + d < n)
            def _():
                pl.semaphore_signal(barrier, inc=1, device_id={"domain": me + d})

        for d in range(1, REACH + 1):

            @pl.when(me >= d)
            def _():
                pl.semaphore_wait(barrier, 1)

            @pl.when(me + d < n)
            def _():
                pl.semaphore_wait(barrier, 1)

    def rows_at(group):
        return pl.ds(group * TILE, TILE)

    sources = (x_ref, x1_ref, x2_ref)

    def x_copy(step, d, group):
        return pltpu.make_async_remote_copy(
            src_ref=sources[step].at[rows_at(group)],
            dst_ref=in_x.at[step, d - 1, rows_at(group)],
            send_sem=xs_sem.at[step, d - 1, group],
            recv_sem=xr_sem.at[step, d - 1, group],
            device_id={"domain": me - d},
        )

    def b_copy(step, d, group):
        return pltpu.make_async_remote_copy(
            src_ref=out_b.at[step, d - 1, rows_at(group)],
            dst_ref=in_b.at[step, d - 1, rows_at(group)],
            send_sem=bs_sem.at[step, d - 1, group],
            recv_sem=br_sem.at[step, d - 1, group],
            device_id={"domain": me + d},
        )

    def send_x(step, group):
        for d in range(1, REACH + 1):

            @pl.when(me >= d)
            def _():
                x_copy(step, d, group).start()

    if with_gram:
        (in_f, part, in_g1, out_g, in_g2, in_h, in_k) = refs[17:24]
        (fs_sem, fr_sem, g1s_sem, g1r_sem, g2s_sem, g2r_sem, hs_sem, hr_sem, ks_sem, kr_sem) = refs[24:]
        far = (mine + 2) % 4
        near = mine + 1 - 2 * (mine % 2)
        cross = (near + 2) % 4

        def f_copy(index, group):
            source = in_f.at[0] if index == 2 else f_ref
            return pltpu.make_async_remote_copy(
                src_ref=source.at[rows_at(group)],
                dst_ref=in_f.at[index, rows_at(group)],
                send_sem=fs_sem.at[index, group],
                recv_sem=fr_sem.at[index, group],
                device_id={"vec": far if index == 0 else near},
            )

    for group in range(groups):
        send_x(0, group)

    both[...] = stacked(x_ref[...])
    load.wait()

    def add_before(slot, carry):
        before = before_ref[slot]
        weight = (before >= 0).astype(F32)
        tiles[slot] = tiles[slot] + tiles[jnp.maximum(before, 0)] * weight
        return carry

    lax.fori_loop(0, tiles.shape[0], add_before, 0)

    def block_at(row, col):
        slot = last_ref[row * span + col]
        return tiles[jnp.maximum(slot, 0)] * (slot >= 0).astype(F32)

    def put(high, low, index, row, col, value):
        high[index, rows_at(row), rows_at(col)], low[index, rows_at(row), rows_at(col)] = halves(value)

    for d in range(1, REACH + 1):
        for row in range(groups):
            for col in range(groups):
                block = block_at(row, d * groups + col)
                put(fwd_h, fwd_l, d, row, col, block)
                put(back_h, back_l, d - 1, col, row, block.T)
    for row in range(groups):
        for col in range(row, groups):
            block = block_at(row, col)
            if row == col:
                put(fwd_h, fwd_l, 0, row, col, 0.5 * (block + block.T))
            else:
                put(fwd_h, fwd_l, 0, row, col, block)
                put(fwd_h, fwd_l, 0, col, row, block.T)

    for step in range(3):
        if step > 0:
            both[...] = stacked(sources[step][...])
        for d in range(1, REACH + 1):

            @pl.when(me + d < n)
            def _():
                out_b[step, d - 1] = product(back_h[d - 1], back_l[d - 1], both[...])

        for group in range(groups):
            for d in range(1, REACH + 1):

                @pl.when(me + d < n)
                def _():
                    b_copy(step, d, group).start()

        acc[...] = product(fwd_h[0], fwd_l[0], both[...])
        for d in range(1, REACH + 1):

            @pl.when(me + d < n)
            def _():
                for group in range(groups):
                    x_copy(step, d, group).wait_recv()
                acc[...] += product(fwd_h[d], fwd_l[d], stacked(in_x[step, d - 1]))

        for group in range(groups):
            here = rows_at(group)
            for d in range(1, REACH + 1):

                @pl.when(me >= d)
                def _():
                    b_copy(step, d, group).wait_recv()
                    acc[here] += in_b[step, d - 1, here]

            if step == 0:
                x1_ref[here] = (acc[here] - center_shift * x_ref[here]) / half_width
            elif step == 1:
                x2_ref[here] = 2.0 * (acc[here] - center_shift * x1_ref[here]) / half_width - x_ref[here]
            else:
                f_ref[here] = 2.0 * (acc[here] - center_shift * x2_ref[here]) / half_width - x1_ref[here]
            if step < 2:
                send_x(step + 1, group)
            elif with_gram:
                f_copy(0, group).start()
                f_copy(1, group).start()

    if with_gram:
        left_h, left_l = halves(f_ref[...].T)
        back_h[0, :width], back_l[0, :width] = left_h, left_l
        total = rows * n

        piece = width // n
        pairs = n // 2
        pair = me // 2
        side = me % 2
        mate = me + 1 - 2 * side
        owners = (mine, near, far, cross)

        def rows_of(owner):
            return pl.ds(pl.multiple_of(owner * piece, piece), piece)

        def at(column, owner):
            return (rows_of(owner), pl.ds(pl.multiple_of(owners[column] * width, width), width))

        def g1_copy(column, d):
            return pltpu.make_async_remote_copy(
                src_ref=part.at[column, rows_of(2 * ((pair + d) % pairs) + 1 - side)],
                dst_ref=in_g1.at[column, d],
                send_sem=g1s_sem.at[column, d],
                recv_sem=g1r_sem.at[column, d],
                device_id={"domain": mate},
            )

        def g2_copy(column, d):
            return pltpu.make_async_remote_copy(
                src_ref=out_g.at[column, d],
                dst_ref=in_g2.at[column, d],
                send_sem=g2s_sem.at[column, d],
                recv_sem=g2r_sem.at[column, d],
                device_id={"domain": 2 * ((pair + d) % pairs) + side},
            )

        def h_copy(column, d):
            return pltpu.make_async_remote_copy(
                src_ref=out_g.at[column, 0],
                dst_ref=in_h.at[column, d],
                send_sem=hs_sem.at[column, d],
                recv_sem=hr_sem.at[column, d],
                device_id={"domain": 2 * ((pair + d) % pairs) + side},
            )

        def k_copy(column, d):
            return pltpu.make_async_remote_copy(
                src_ref=out_g.at[column, 0] if d == 0 else in_h.at[column, d],
                dst_ref=in_k.at[column, d],
                send_sem=ks_sem.at[column, d],
                recv_sem=kr_sem.at[column, d],
                device_id={"domain": mate},
            )

        order = list(range(1, pairs)) + [0]

        def multiply(column, value):
            block = product(back_h[0, :width], back_l[0, :width], stacked(value)) / total
            part[column] = block
            for d in order:
                g1_copy(column, d).start()

        def add_mate(column):
            for d in order:
                g1_copy(column, d).wait_recv()
                out_g[column, d] = part[column, rows_of(2 * ((pair + d) % pairs) + side)] + in_g1[column, d]
                if d > 0:
                    g2_copy(column, d).start()

        def add_pairs(column):
            block = out_g[column, 0]
            for d in range(1, pairs):
                g2_copy(column, d).wait_recv()
                block = block + in_g2[column, d]
            out_g[column, 0] = block
            for d in range(1, pairs):
                h_copy(column, d).start()
            k_copy(column, 0).start()
            g_ref[at(column, me)] = block

        def from_pairs(column):
            for d in range(1, pairs):
                h_copy(column, d).wait_recv()
                k_copy(column, d).start()
                g_ref[at(column, 2 * ((pair + pairs - d) % pairs) + side)] = in_h[column, d]

        def from_mate(column):
            for d in range(pairs):
                k_copy(column, d).wait_recv()
                g_ref[at(column, 2 * ((pair + pairs - d) % pairs) + 1 - side)] = in_k[column, d]

        multiply(0, f_ref[...])
        for group in range(groups):
            f_copy(1, group).wait_recv()
        multiply(1, in_f[1])
        for group in range(groups):
            f_copy(0, group).wait_recv()
            f_copy(2, group).start()
        multiply(2, in_f[0])
        add_mate(0)
        add_mate(1)
        for group in range(groups):
            f_copy(2, group).wait_recv()
        multiply(3, in_f[2])
        add_mate(2)
        add_pairs(0)
        add_pairs(1)
        add_mate(3)
        add_pairs(2)
        from_pairs(0)
        from_pairs(1)
        add_pairs(3)
        from_pairs(2)
        from_mate(0)
        from_mate(1)
        from_pairs(3)
        from_mate(2)
        from_mate(3)
        for group in range(groups):
            for index in range(3):
                f_copy(index, group).wait_send()
        for column in range(4):
            for d in range(pairs):
                g1_copy(column, d).wait_send()
                k_copy(column, d).wait_send()
            for d in range(1, pairs):
                g2_copy(column, d).wait_send()
                h_copy(column, d).wait_send()

    for step in range(3):
        for d in range(1, REACH + 1):

            @pl.when(me >= d)
            def _():
                for group in range(groups):
                    x_copy(step, d, group).wait_send()

            @pl.when(me + d < n)
            def _():
                for group in range(groups):
                    b_copy(step, d, group).wait_send()


def shards(vectors, hamiltonian, tile_pairs, tile_counts):
    n = lax.axis_size("domain")
    m = lax.axis_size("vec")
    rows, width = vectors.shape
    groups = rows // TILE
    before, last = index_slots(tile_pairs, tile_counts, groups)
    with_gram = m == 4 and n % 2 == 0 and width % (8 * n) == 0
    dma = pltpu.SemaphoreType.DMA
    out_shape = [jax.ShapeDtypeStruct((rows, width), F32)]
    scratch = [
        pltpu.VMEM(hamiltonian.shape, F32),
        pltpu.VMEM((REACH + 1, rows, rows), BF16),
        pltpu.VMEM((REACH + 1, rows, rows), BF16),
        pltpu.VMEM((REACH, rows, rows), BF16),
        pltpu.VMEM((REACH, rows, rows), BF16),
        pltpu.VMEM((rows, 2 * width), BF16),
        pltpu.VMEM((rows, width), F32),
        pltpu.VMEM((rows, width), F32),
        pltpu.VMEM((rows, width), F32),
        pltpu.VMEM((3, REACH, rows, width), F32),
        pltpu.VMEM((3, REACH, rows, width), F32),
        pltpu.VMEM((3, REACH, rows, width), F32),
        dma,
        dma((3, REACH, groups)),
        dma((3, REACH, groups)),
        dma((3, REACH, groups)),
        dma((3, REACH, groups)),
    ]
    if with_gram:
        out_shape.append(jax.ShapeDtypeStruct((width, m * width), F32))
        scratch += [
            pltpu.VMEM((3, rows, width), F32),
            pltpu.VMEM((m, width, width), F32),
            dma((3, groups)),
            dma((3, groups)),
        ]
        scratch[-2:-2] = [pltpu.VMEM((m, n // 2, width // n, width), F32)] * 5
        scratch += [dma((m, n // 2))] * 8
    outs = pl.pallas_call(
        functools.partial(filter_kernel, n, m, with_gram),
        out_shape=out_shape,
        in_specs=[
            pl.BlockSpec(memory_space=pltpu.VMEM),
            pl.BlockSpec(memory_space=pltpu.SMEM),
            pl.BlockSpec(memory_space=pltpu.SMEM),
            pl.BlockSpec(memory_space=pl.ANY),
        ],
        out_specs=[pl.BlockSpec(memory_space=pltpu.VMEM)] * len(out_shape),
        scratch_shapes=scratch,
        compiler_params=pltpu.CompilerParams(
            collective_id=0, has_side_effects=True, vmem_limit_bytes=52 * 2**20
        ),
        name="chebyshev",
    )(vectors, before, last, hamiltonian)
    if with_gram:
        return tuple(outs)
    (filtered,) = outs
    gathered = lax.all_gather(filtered, "vec", axis=1, tiled=True)
    partial_block = jnp.dot(
        filtered.T, gathered, precision=lax.Precision.HIGHEST, preferred_element_type=F32
    ) / (rows * n)
    return (filtered, lax.psum(partial_block, "domain"))


def solution(mesh):
    in_specs = (P("domain", "vec"), P("domain", None, None), P("domain", None), P("domain"))
    out_specs = (P("domain", "vec"), P("vec", None))
    return jax.shard_map(shards, mesh=mesh, in_specs=in_specs, out_specs=out_specs, check_vma=False)
```

```python
import functools

import jax
import jax.numpy as jnp
from jax import lax
from jax.experimental import pallas as pl
from jax.experimental.pallas import tpu as pltpu
from jax.sharding import PartitionSpec as P

TILE = 128
REACH = 2

center_shift = 1.0
half_width = 1.5

F32 = jnp.float32
BF16 = jnp.bfloat16


def index_kernel(groups, span, pairs_ref, count_ref, before_ref, last_ref):
    slots = pairs_ref.shape[1]
    count = count_ref[0]
    base = lax.axis_index("domain") * groups

    def clear(block, carry):
        last_ref[block] = -1
        return carry

    def chain(slot, carry):
        block = (pairs_ref[0, slot] - base) * span + pairs_ref[1, slot] - base
        before_ref[slot] = last_ref[block]
        last_ref[block] = slot
        return carry

    def skip(slot, carry):
        before_ref[slot] = -1
        return carry

    lax.fori_loop(0, groups * span, clear, 0)
    lax.fori_loop(0, count, chain, 0)
    lax.fori_loop(count, slots, skip, 0)


def index_slots(tile_pairs, tile_counts, groups):
    span = (REACH + 1) * groups
    smem = pl.BlockSpec(memory_space=pltpu.SMEM)
    return pl.pallas_call(
        functools.partial(index_kernel, groups, span),
        out_shape=[
            jax.ShapeDtypeStruct((tile_pairs.shape[0],), jnp.int32),
            jax.ShapeDtypeStruct((groups * span,), jnp.int32),
        ],
        in_specs=[smem, smem],
        out_specs=[smem, smem],
        name="index_slots",
    )(tile_pairs.T, tile_counts)


def halves(value):
    high = value.astype(BF16)
    low = (value - high.astype(F32)).astype(BF16)
    return high, low


def stacked(value):
    return jnp.concatenate(halves(value), 1)


def product(high, low, both):
    wide = jnp.dot(high, both, preferred_element_type=F32)
    wide = wide + jnp.dot(low, both, preferred_element_type=F32)
    width = both.shape[1] // 2
    return wide[:, :width] + wide[:, width:]


def filter_kernel(n, m, with_gram, x_ref, before_ref, last_ref, ham_ref, *refs):
    if with_gram:
        f_ref, g_ref, *refs = refs
    else:
        f_ref, *refs = refs
    (tiles, fwd_h, fwd_l, back_h, back_l, both, acc, x1_ref, x2_ref, in_x, in_b, out_b) = refs[:12]
    (load_sem, xs_sem, xr_sem, bs_sem, br_sem) = refs[12:17]
    me = lax.axis_index("domain")
    mine = lax.axis_index("vec")
    rows, width = x_ref.shape
    groups = rows // TILE
    span = (REACH + 1) * groups

    load = pltpu.make_async_copy(ham_ref, tiles, load_sem)
    load.start()

    barrier = pltpu.get_barrier_semaphore()
    if with_gram:
        for d in range(1, n):
            pl.semaphore_signal(barrier, inc=1, device_id={"domain": (me + d) % n})
        for d in range(1, m):
            pl.semaphore_signal(barrier, inc=1, device_id={"vec": (mine + d) % m})
        pl.semaphore_wait(barrier, n - 1 + m - 1)
    else:
        for d in range(1, REACH + 1):

            @pl.when(me >= d)
            def _():
                pl.semaphore_signal(barrier, inc=1, device_id={"domain": me - d})

            @pl.when(me + d < n)
            def _():
                pl.semaphore_signal(barrier, inc=1, device_id={"domain": me + d})

        for d in range(1, REACH + 1):

            @pl.when(me >= d)
            def _():
                pl.semaphore_wait(barrier, 1)

            @pl.when(me + d < n)
            def _():
                pl.semaphore_wait(barrier, 1)

    def rows_at(group):
        return pl.ds(group * TILE, TILE)

    sources = (x_ref, x1_ref, x2_ref)

    def x_copy(step, d, group):
        return pltpu.make_async_remote_copy(
            src_ref=sources[step].at[rows_at(group)],
            dst_ref=in_x.at[step, d - 1, rows_at(group)],
            send_sem=xs_sem.at[step, d - 1, group],
            recv_sem=xr_sem.at[step, d - 1, group],
            device_id={"domain": me - d},
        )

    def b_copy(step, d, group):
        return pltpu.make_async_remote_copy(
            src_ref=out_b.at[step, d - 1, rows_at(group)],
            dst_ref=in_b.at[step, d - 1, rows_at(group)],
            send_sem=bs_sem.at[step, d - 1, group],
            recv_sem=br_sem.at[step, d - 1, group],
            device_id={"domain": me + d},
        )

    relayed = n % 2 == 0 and REACH == 2
    even = me % 2 == 0

    def x_relay(step, group):
        return pltpu.make_async_remote_copy(
            src_ref=in_x.at[step, 1, rows_at(group)],
            dst_ref=in_x.at[step, 0, rows_at(group)],
            send_sem=xs_sem.at[step, 0, group],
            recv_sem=xr_sem.at[step, 0, group],
            device_id={"domain": me + 1},
        )

    def sends_x(d):
        return jnp.logical_and(me >= d, me % 2 == 1) if relayed and d == 1 else me >= d

    def send_x(step, group):
        for d in range(1, REACH + 1):

            @pl.when(sends_x(d))
            def _():
                x_copy(step, d, group).start()

    if with_gram:
        (in_f, part, in_g1, out_g, in_g2, in_h, in_k) = refs[17:24]
        (fs_sem, fr_sem, g1s_sem, g1r_sem, g2s_sem, g2r_sem, hs_sem, hr_sem, ks_sem, kr_sem) = refs[24:]
        far = (mine + 2) % 4
        near = mine + 1 - 2 * (mine % 2)
        cross = (near + 2) % 4

        def f_copy(index, group):
            source = in_f.at[0] if index == 2 else f_ref
            return pltpu.make_async_remote_copy(
                src_ref=source.at[rows_at(group)],
                dst_ref=in_f.at[index, rows_at(group)],
                send_sem=fs_sem.at[index, group],
                recv_sem=fr_sem.at[index, group],
                device_id={"vec": far if index == 0 else near},
            )

    for group in range(groups):
        send_x(0, group)

    both[...] = stacked(x_ref[...])
    load.wait()

    def add_before(slot, carry):
        before = before_ref[slot]
        weight = (before >= 0).astype(F32)
        tiles[slot] = tiles[slot] + tiles[jnp.maximum(before, 0)] * weight
        return carry

    lax.fori_loop(0, tiles.shape[0], add_before, 0)

    def block_at(row, col):
        slot = last_ref[row * span + col]
        return tiles[jnp.maximum(slot, 0)] * (slot >= 0).astype(F32)

    def put(high, low, index, row, col, value):
        high[index, rows_at(row), rows_at(col)], low[index, rows_at(row), rows_at(col)] = halves(value)

    for d in range(1, REACH + 1):
        for row in range(groups):
            for col in range(groups):
                block = block_at(row, d * groups + col)
                put(fwd_h, fwd_l, d, row, col, block)
                put(back_h, back_l, d - 1, col, row, block.T)
    for row in range(groups):
        for col in range(row, groups):
            block = block_at(row, col)
            if row == col:
                put(fwd_h, fwd_l, 0, row, col, 0.5 * (block + block.T))
            else:
                put(fwd_h, fwd_l, 0, row, col, block)
                put(fwd_h, fwd_l, 0, col, row, block.T)

    for step in range(3):
        if step > 0:
            both[...] = stacked(sources[step][...])
        for d in range(1, REACH + 1):

            @pl.when(me + d < n)
            def _():
                out_b[step, d - 1] = product(back_h[d - 1], back_l[d - 1], both[...])

        def send_back(first, last):
            for group in range(first, last):
                for d in range(1, REACH + 1):

                    @pl.when(me + d < n)
                    def _():
                        b_copy(step, d, group).start()

        send_back(0, groups // 2)
        acc[...] = product(fwd_h[0], fwd_l[0], both[...])
        if relayed:

            @pl.when(jnp.logical_and(even, me + 2 < n))
            def _():
                for group in range(groups):
                    x_copy(step, 2, group).wait_recv()
                    x_relay(step, group).start()

        send_back(groups // 2, groups)
        for d in range(REACH, 0, -1):
            if relayed and d == 2:
                waits = jnp.logical_and(me % 2 == 1, me + d < n)
            else:
                waits = me + d < n

            @pl.when(waits)
            def _():
                for group in range(groups):
                    x_copy(step, d, group).wait_recv()

            @pl.when(me + d < n)
            def _():
                acc[...] += product(fwd_h[d], fwd_l[d], stacked(in_x[step, d - 1]))

        for group in range(groups):
            here = rows_at(group)
            for d in range(1, REACH + 1):

                @pl.when(me >= d)
                def _():
                    b_copy(step, d, group).wait_recv()
                    acc[here] += in_b[step, d - 1, here]

            if step == 0:
                x1_ref[here] = (acc[here] - center_shift * x_ref[here]) / half_width
            elif step == 1:
                x2_ref[here] = 2.0 * (acc[here] - center_shift * x1_ref[here]) / half_width - x_ref[here]
            else:
                f_ref[here] = 2.0 * (acc[here] - center_shift * x2_ref[here]) / half_width - x1_ref[here]
            if step < 2:
                send_x(step + 1, group)
            elif with_gram:
                f_copy(0, group).start()
                f_copy(1, group).start()

    if with_gram:
        left_h, left_l = halves(f_ref[...].T)
        back_h[0, :width], back_l[0, :width] = left_h, left_l
        total = rows * n

        piece = width // n
        pairs = n // 2
        pair = me // 2
        side = me % 2
        mate = me + 1 - 2 * side
        owners = (mine, near, far, cross)

        def rows_of(owner):
            return pl.ds(pl.multiple_of(owner * piece, piece), piece)

        def at(column, owner):
            return (rows_of(owner), pl.ds(pl.multiple_of(owners[column] * width, width), width))

        def g1_copy(column, d):
            return pltpu.make_async_remote_copy(
                src_ref=part.at[column, rows_of(2 * ((pair + d) % pairs) + 1 - side)],
                dst_ref=in_g1.at[column, d],
                send_sem=g1s_sem.at[column, d],
                recv_sem=g1r_sem.at[column, d],
                device_id={"domain": mate},
            )

        def g2_copy(column, d):
            return pltpu.make_async_remote_copy(
                src_ref=out_g.at[column, d],
                dst_ref=in_g2.at[column, d],
                send_sem=g2s_sem.at[column, d],
                recv_sem=g2r_sem.at[column, d],
                device_id={"domain": 2 * ((pair + d) % pairs) + side},
            )

        def h_copy(column, d):
            return pltpu.make_async_remote_copy(
                src_ref=out_g.at[column, 0],
                dst_ref=in_h.at[column, d],
                send_sem=hs_sem.at[column, d],
                recv_sem=hr_sem.at[column, d],
                device_id={"domain": 2 * ((pair + d) % pairs) + side},
            )

        def k_copy(column, d):
            return pltpu.make_async_remote_copy(
                src_ref=out_g.at[column, 0] if d == 0 else in_h.at[column, d],
                dst_ref=in_k.at[column, d],
                send_sem=ks_sem.at[column, d],
                recv_sem=kr_sem.at[column, d],
                device_id={"domain": mate},
            )

        order = list(range(1, pairs)) + [0]

        def multiply(column, value):
            block = product(back_h[0, :width], back_l[0, :width], stacked(value)) / total
            part[column] = block
            for d in order:
                g1_copy(column, d).start()

        def add_mate(column):
            for d in order:
                g1_copy(column, d).wait_recv()
                out_g[column, d] = part[column, rows_of(2 * ((pair + d) % pairs) + side)] + in_g1[column, d]
                if d > 0:
                    g2_copy(column, d).start()

        def add_pairs(column):
            block = out_g[column, 0]
            for d in range(1, pairs):
                g2_copy(column, d).wait_recv()
                block = block + in_g2[column, d]
            out_g[column, 0] = block
            for d in range(1, pairs):
                h_copy(column, d).start()
            k_copy(column, 0).start()
            g_ref[at(column, me)] = block

        def from_pairs(column):
            for d in range(1, pairs):
                h_copy(column, d).wait_recv()
                k_copy(column, d).start()
                g_ref[at(column, 2 * ((pair + pairs - d) % pairs) + side)] = in_h[column, d]

        def from_mate(column):
            for d in range(pairs):
                k_copy(column, d).wait_recv()
                g_ref[at(column, 2 * ((pair + pairs - d) % pairs) + 1 - side)] = in_k[column, d]

        multiply(0, f_ref[...])
        for group in range(groups):
            f_copy(1, group).wait_recv()
        multiply(1, in_f[1])
        for group in range(groups):
            f_copy(0, group).wait_recv()
            f_copy(2, group).start()
        multiply(2, in_f[0])
        add_mate(0)
        add_mate(1)
        for group in range(groups):
            f_copy(2, group).wait_recv()
        multiply(3, in_f[2])
        add_mate(2)
        add_pairs(0)
        add_pairs(1)
        add_mate(3)
        add_pairs(2)
        from_pairs(0)
        from_pairs(1)
        add_pairs(3)
        from_pairs(2)
        from_mate(0)
        from_mate(1)
        from_pairs(3)
        from_mate(2)
        from_mate(3)
        for group in range(groups):
            for index in range(3):
                f_copy(index, group).wait_send()
        for column in range(4):
            for d in range(pairs):
                g1_copy(column, d).wait_send()
                k_copy(column, d).wait_send()
            for d in range(1, pairs):
                g2_copy(column, d).wait_send()
                h_copy(column, d).wait_send()

    for step in range(3):
        if relayed:

            @pl.when(jnp.logical_and(even, me + 2 < n))
            def _():
                for group in range(groups):
                    x_relay(step, group).wait_send()

        for d in range(1, REACH + 1):

            @pl.when(sends_x(d))
            def _():
                for group in range(groups):
                    x_copy(step, d, group).wait_send()

            @pl.when(me + d < n)
            def _():
                for group in range(groups):
                    b_copy(step, d, group).wait_send()


def shards(vectors, hamiltonian, tile_pairs, tile_counts):
    n = lax.axis_size("domain")
    m = lax.axis_size("vec")
    rows, width = vectors.shape
    groups = rows // TILE
    before, last = index_slots(tile_pairs, tile_counts, groups)
    with_gram = m == 4 and n % 2 == 0 and width % (8 * n) == 0
    dma = pltpu.SemaphoreType.DMA
    out_shape = [jax.ShapeDtypeStruct((rows, width), F32)]
    scratch = [
        pltpu.VMEM(hamiltonian.shape, F32),
        pltpu.VMEM((REACH + 1, rows, rows), BF16),
        pltpu.VMEM((REACH + 1, rows, rows), BF16),
        pltpu.VMEM((REACH, rows, rows), BF16),
        pltpu.VMEM((REACH, rows, rows), BF16),
        pltpu.VMEM((rows, 2 * width), BF16),
        pltpu.VMEM((rows, width), F32),
        pltpu.VMEM((rows, width), F32),
        pltpu.VMEM((rows, width), F32),
        pltpu.VMEM((3, REACH, rows, width), F32),
        pltpu.VMEM((3, REACH, rows, width), F32),
        pltpu.VMEM((3, REACH, rows, width), F32),
        dma,
        dma((3, REACH, groups)),
        dma((3, REACH, groups)),
        dma((3, REACH, groups)),
        dma((3, REACH, groups)),
    ]
    if with_gram:
        out_shape.append(jax.ShapeDtypeStruct((width, m * width), F32))
        scratch += [
            pltpu.VMEM((3, rows, width), F32),
            pltpu.VMEM((m, width, width), F32),
            dma((3, groups)),
            dma((3, groups)),
        ]
        scratch[-2:-2] = [pltpu.VMEM((m, n // 2, width // n, width), F32)] * 5
        scratch += [dma((m, n // 2))] * 8
    outs = pl.pallas_call(
        functools.partial(filter_kernel, n, m, with_gram),
        out_shape=out_shape,
        in_specs=[
            pl.BlockSpec(memory_space=pltpu.VMEM),
            pl.BlockSpec(memory_space=pltpu.SMEM),
            pl.BlockSpec(memory_space=pltpu.SMEM),
            pl.BlockSpec(memory_space=pl.ANY),
        ],
        out_specs=[pl.BlockSpec(memory_space=pltpu.VMEM)] * len(out_shape),
        scratch_shapes=scratch,
        compiler_params=pltpu.CompilerParams(
            collective_id=0, has_side_effects=True, vmem_limit_bytes=52 * 2**20
        ),
        name="chebyshev",
    )(vectors, before, last, hamiltonian)
    if with_gram:
        return tuple(outs)
    (filtered,) = outs
    gathered = lax.all_gather(filtered, "vec", axis=1, tiled=True)
    partial_block = jnp.dot(
        filtered.T, gathered, precision=lax.Precision.HIGHEST, preferred_element_type=F32
    ) / (rows * n)
    return (filtered, lax.psum(partial_block, "domain"))


def solution(mesh):
    in_specs = (P("domain", "vec"), P("domain", None, None), P("domain", None), P("domain"))
    out_specs = (P("domain", "vec"), P("vec", None))
    return jax.shard_map(shards, mesh=mesh, in_specs=in_specs, out_specs=out_specs, check_vma=False)
```

```python
import functools

import jax
import jax.numpy as jnp
from jax import lax
from jax.experimental import pallas as pl
from jax.experimental.pallas import tpu as pltpu
from jax.sharding import PartitionSpec as P

TILE = 128
REACH = 2

center_shift = 1.0
half_width = 1.5

F32 = jnp.float32
BF16 = jnp.bfloat16


def index_kernel(groups, span, pairs_ref, count_ref, before_ref, last_ref):
    slots = pairs_ref.shape[1]
    count = count_ref[0]
    base = lax.axis_index("domain") * groups

    def clear(block, carry):
        last_ref[block] = -1
        return carry

    def chain(slot, carry):
        block = (pairs_ref[0, slot] - base) * span + pairs_ref[1, slot] - base
        before_ref[slot] = last_ref[block]
        last_ref[block] = slot
        return carry

    def skip(slot, carry):
        before_ref[slot] = -1
        return carry

    lax.fori_loop(0, groups * span, clear, 0)
    lax.fori_loop(0, count, chain, 0)
    lax.fori_loop(count, slots, skip, 0)


def index_slots(tile_pairs, tile_counts, groups):
    span = (REACH + 1) * groups
    smem = pl.BlockSpec(memory_space=pltpu.SMEM)
    return pl.pallas_call(
        functools.partial(index_kernel, groups, span),
        out_shape=[
            jax.ShapeDtypeStruct((tile_pairs.shape[0],), jnp.int32),
            jax.ShapeDtypeStruct((groups * span,), jnp.int32),
        ],
        in_specs=[smem, smem],
        out_specs=[smem, smem],
        name="index_slots",
    )(tile_pairs.T, tile_counts)


def halves(value):
    high = value.astype(BF16)
    low = (value - high.astype(F32)).astype(BF16)
    return high, low


def stacked(value):
    return jnp.concatenate(halves(value), 1)


def product(high, low, both):
    wide = jnp.dot(high, both, preferred_element_type=F32)
    wide = wide + jnp.dot(low, both, preferred_element_type=F32)
    width = both.shape[1] // 2
    return wide[:, :width] + wide[:, width:]


def filter_kernel(n, m, with_gram, x_ref, before_ref, last_ref, ham_ref, *refs):
    if with_gram:
        f_ref, g_ref, *refs = refs
    else:
        f_ref, *refs = refs
    (tiles, fwd_h, fwd_l, back_h, back_l, both, acc, x1_ref, x2_ref, in_x, in_b, out_b) = refs[:12]
    (load_sem, xs_sem, xr_sem, bs_sem, br_sem) = refs[12:17]
    me = lax.axis_index("domain")
    mine = lax.axis_index("vec")
    rows, width = x_ref.shape
    groups = rows // TILE
    span = (REACH + 1) * groups

    load = pltpu.make_async_copy(ham_ref, tiles, load_sem)
    load.start()

    barrier = pltpu.get_barrier_semaphore()
    if with_gram:
        for d in range(1, n):
            pl.semaphore_signal(barrier, inc=1, device_id={"domain": (me + d) % n})
        for d in range(1, m):
            pl.semaphore_signal(barrier, inc=1, device_id={"vec": (mine + d) % m})
        pl.semaphore_wait(barrier, n - 1 + m - 1)
    else:
        for d in range(1, REACH + 1):

            @pl.when(me >= d)
            def _():
                pl.semaphore_signal(barrier, inc=1, device_id={"domain": me - d})

            @pl.when(me + d < n)
            def _():
                pl.semaphore_signal(barrier, inc=1, device_id={"domain": me + d})

        for d in range(1, REACH + 1):

            @pl.when(me >= d)
            def _():
                pl.semaphore_wait(barrier, 1)

            @pl.when(me + d < n)
            def _():
                pl.semaphore_wait(barrier, 1)

    def rows_at(group):
        return pl.ds(group * TILE, TILE)

    sources = (x_ref, x1_ref, x2_ref)

    def x_copy(step, d, group):
        return pltpu.make_async_remote_copy(
            src_ref=sources[step].at[rows_at(group)],
            dst_ref=in_x.at[step, d - 1, rows_at(group)],
            send_sem=xs_sem.at[step, d - 1, group],
            recv_sem=xr_sem.at[step, d - 1, group],
            device_id={"domain": me - d},
        )

    def b_copy(step, d, group):
        return pltpu.make_async_remote_copy(
            src_ref=out_b.at[step, d - 1, rows_at(group)],
            dst_ref=in_b.at[step, d - 1, rows_at(group)],
            send_sem=bs_sem.at[step, d - 1, group],
            recv_sem=br_sem.at[step, d - 1, group],
            device_id={"domain": me + d},
        )

    def send_x(step, d, group):
        @pl.when(me >= d)
        def _():
            x_copy(step, d, group).start()

    def send_x_far(step):
        for d in range(2, REACH + 1):
            for group in range(groups):
                send_x(step, d, group)

    if with_gram:
        (in_f, part, in_g1, out_g, in_g2, in_h, in_k) = refs[17:24]
        (fs_sem, fr_sem, g1s_sem, g1r_sem, g2s_sem, g2r_sem, hs_sem, hr_sem, ks_sem, kr_sem) = refs[24:]
        far = (mine + 2) % 4
        near = mine + 1 - 2 * (mine % 2)
        cross = (near + 2) % 4

        def f_copy(index, group):
            source = in_f.at[0] if index == 2 else f_ref
            return pltpu.make_async_remote_copy(
                src_ref=source.at[rows_at(group)],
                dst_ref=in_f.at[index, rows_at(group)],
                send_sem=fs_sem.at[index, group],
                recv_sem=fr_sem.at[index, group],
                device_id={"vec": far if index == 0 else near},
            )

    for group in range(groups):
        send_x(0, 1, group)
    send_x_far(0)

    both[...] = stacked(x_ref[...])
    load.wait()

    def add_before(slot, carry):
        before = before_ref[slot]
        weight = (before >= 0).astype(F32)
        tiles[slot] = tiles[slot] + tiles[jnp.maximum(before, 0)] * weight
        return carry

    lax.fori_loop(0, tiles.shape[0], add_before, 0)

    def block_at(row, col):
        slot = last_ref[row * span + col]
        return tiles[jnp.maximum(slot, 0)] * (slot >= 0).astype(F32)

    def put(high, low, index, row, col, value):
        high[index, rows_at(row), rows_at(col)], low[index, rows_at(row), rows_at(col)] = halves(value)

    for d in range(1, REACH + 1):
        for row in range(groups):
            for col in range(groups):
                block = block_at(row, d * groups + col)
                put(fwd_h, fwd_l, d, row, col, block)
                put(back_h, back_l, d - 1, col, row, block.T)
    for row in range(groups):
        for col in range(row, groups):
            block = block_at(row, col)
            if row == col:
                put(fwd_h, fwd_l, 0, row, col, 0.5 * (block + block.T))
            else:
                put(fwd_h, fwd_l, 0, row, col, block)
                put(fwd_h, fwd_l, 0, col, row, block.T)

    for step in range(3):
        if step > 0:
            both[...] = stacked(sources[step][...])
        for d in range(1, REACH + 1):

            @pl.when(me + d < n)
            def _():
                out_b[step, d - 1] = product(back_h[d - 1], back_l[d - 1], both[...])

        for group in range(groups):
            for d in range(1, REACH + 1):

                @pl.when(me + d < n)
                def _():
                    b_copy(step, d, group).start()

        acc[...] = product(fwd_h[0], fwd_l[0], both[...])
        for d in range(1, REACH + 1):

            @pl.when(me + d < n)
            def _():
                for group in range(groups):
                    x_copy(step, d, group).wait_recv()
                acc[...] += product(fwd_h[d], fwd_l[d], stacked(in_x[step, d - 1]))

        for group in range(groups):
            here = rows_at(group)
            for d in range(1, REACH + 1):

                @pl.when(me >= d)
                def _():
                    b_copy(step, d, group).wait_recv()
                    acc[here] += in_b[step, d - 1, here]

            if step == 0:
                x1_ref[here] = (acc[here] - center_shift * x_ref[here]) / half_width
            elif step == 1:
                x2_ref[here] = 2.0 * (acc[here] - center_shift * x1_ref[here]) / half_width - x_ref[here]
            else:
                f_ref[here] = 2.0 * (acc[here] - center_shift * x2_ref[here]) / half_width - x1_ref[here]
            if step < 2:
                send_x(step + 1, 1, group)
            elif with_gram:
                f_copy(0, group).start()
                f_copy(1, group).start()
        if step < 2:
            send_x_far(step + 1)

    if with_gram:
        left_h, left_l = halves(f_ref[...].T)
        back_h[0, :width], back_l[0, :width] = left_h, left_l
        total = rows * n

        piece = width // n
        pairs = n // 2
        pair = me // 2
        side = me % 2
        mate = me + 1 - 2 * side
        owners = (mine, near, far, cross)

        def rows_of(owner):
            return pl.ds(pl.multiple_of(owner * piece, piece), piece)

        def at(column, owner):
            return (rows_of(owner), pl.ds(pl.multiple_of(owners[column] * width, width), width))

        def g1_copy(column, d):
            return pltpu.make_async_remote_copy(
                src_ref=part.at[column, rows_of(2 * ((pair + d) % pairs) + 1 - side)],
                dst_ref=in_g1.at[column, d],
                send_sem=g1s_sem.at[column, d],
                recv_sem=g1r_sem.at[column, d],
                device_id={"domain": mate},
            )

        def g2_copy(column, d):
            return pltpu.make_async_remote_copy(
                src_ref=out_g.at[column, d],
                dst_ref=in_g2.at[column, d],
                send_sem=g2s_sem.at[column, d],
                recv_sem=g2r_sem.at[column, d],
                device_id={"domain": 2 * ((pair + d) % pairs) + side},
            )

        def h_copy(column, d):
            return pltpu.make_async_remote_copy(
                src_ref=out_g.at[column, 0],
                dst_ref=in_h.at[column, d],
                send_sem=hs_sem.at[column, d],
                recv_sem=hr_sem.at[column, d],
                device_id={"domain": 2 * ((pair + d) % pairs) + side},
            )

        def k_copy(column, d):
            return pltpu.make_async_remote_copy(
                src_ref=out_g.at[column, 0] if d == 0 else in_h.at[column, d],
                dst_ref=in_k.at[column, d],
                send_sem=ks_sem.at[column, d],
                recv_sem=kr_sem.at[column, d],
                device_id={"domain": mate},
            )

        order = list(range(1, pairs)) + [0]

        def multiply(column, value):
            block = product(back_h[0, :width], back_l[0, :width], stacked(value)) / total
            part[column] = block
            for d in order:
                g1_copy(column, d).start()

        def add_mate(column):
            for d in order:
                g1_copy(column, d).wait_recv()
                out_g[column, d] = part[column, rows_of(2 * ((pair + d) % pairs) + side)] + in_g1[column, d]
                if d > 0:
                    g2_copy(column, d).start()

        def add_pairs(column):
            block = out_g[column, 0]
            for d in range(1, pairs):
                g2_copy(column, d).wait_recv()
                block = block + in_g2[column, d]
            out_g[column, 0] = block
            for d in range(1, pairs):
                h_copy(column, d).start()
            k_copy(column, 0).start()
            g_ref[at(column, me)] = block

        def from_pairs(column):
            for d in range(1, pairs):
                h_copy(column, d).wait_recv()
                k_copy(column, d).start()
                g_ref[at(column, 2 * ((pair + pairs - d) % pairs) + side)] = in_h[column, d]

        def from_mate(column):
            for d in range(pairs):
                k_copy(column, d).wait_recv()
                g_ref[at(column, 2 * ((pair + pairs - d) % pairs) + 1 - side)] = in_k[column, d]

        multiply(0, f_ref[...])
        for group in range(groups):
            f_copy(1, group).wait_recv()
        multiply(1, in_f[1])
        for group in range(groups):
            f_copy(0, group).wait_recv()
            f_copy(2, group).start()
        multiply(2, in_f[0])
        add_mate(0)
        add_mate(1)
        for group in range(groups):
            f_copy(2, group).wait_recv()
        multiply(3, in_f[2])
        add_mate(2)
        add_pairs(0)
        add_pairs(1)
        add_mate(3)
        add_pairs(2)
        from_pairs(0)
        from_pairs(1)
        add_pairs(3)
        from_pairs(2)
        from_mate(0)
        from_mate(1)
        from_pairs(3)
        from_mate(2)
        from_mate(3)
        for group in range(groups):
            for index in range(3):
                f_copy(index, group).wait_send()
        for column in range(4):
            for d in range(pairs):
                g1_copy(column, d).wait_send()
                k_copy(column, d).wait_send()
            for d in range(1, pairs):
                g2_copy(column, d).wait_send()
                h_copy(column, d).wait_send()

    for step in range(3):
        for d in range(1, REACH + 1):

            @pl.when(me >= d)
            def _():
                for group in range(groups):
                    x_copy(step, d, group).wait_send()

            @pl.when(me + d < n)
            def _():
                for group in range(groups):
                    b_copy(step, d, group).wait_send()


def shards(vectors, hamiltonian, tile_pairs, tile_counts):
    n = lax.axis_size("domain")
    m = lax.axis_size("vec")
    rows, width = vectors.shape
    groups = rows // TILE
    before, last = index_slots(tile_pairs, tile_counts, groups)
    with_gram = m == 4 and n % 2 == 0 and width % (8 * n) == 0
    dma = pltpu.SemaphoreType.DMA
    out_shape = [jax.ShapeDtypeStruct((rows, width), F32)]
    scratch = [
        pltpu.VMEM(hamiltonian.shape, F32),
        pltpu.VMEM((REACH + 1, rows, rows), BF16),
        pltpu.VMEM((REACH + 1, rows, rows), BF16),
        pltpu.VMEM((REACH, rows, rows), BF16),
        pltpu.VMEM((REACH, rows, rows), BF16),
        pltpu.VMEM((rows, 2 * width), BF16),
        pltpu.VMEM((rows, width), F32),
        pltpu.VMEM((rows, width), F32),
        pltpu.VMEM((rows, width), F32),
        pltpu.VMEM((3, REACH, rows, width), F32),
        pltpu.VMEM((3, REACH, rows, width), F32),
        pltpu.VMEM((3, REACH, rows, width), F32),
        dma,
        dma((3, REACH, groups)),
        dma((3, REACH, groups)),
        dma((3, REACH, groups)),
        dma((3, REACH, groups)),
    ]
    if with_gram:
        out_shape.append(jax.ShapeDtypeStruct((width, m * width), F32))
        scratch += [
            pltpu.VMEM((3, rows, width), F32),
            pltpu.VMEM((m, width, width), F32),
            dma((3, groups)),
            dma((3, groups)),
        ]
        scratch[-2:-2] = [pltpu.VMEM((m, n // 2, width // n, width), F32)] * 5
        scratch += [dma((m, n // 2))] * 8
    outs = pl.pallas_call(
        functools.partial(filter_kernel, n, m, with_gram),
        out_shape=out_shape,
        in_specs=[
            pl.BlockSpec(memory_space=pltpu.VMEM),
            pl.BlockSpec(memory_space=pltpu.SMEM),
            pl.BlockSpec(memory_space=pltpu.SMEM),
            pl.BlockSpec(memory_space=pl.ANY),
        ],
        out_specs=[pl.BlockSpec(memory_space=pltpu.VMEM)] * len(out_shape),
        scratch_shapes=scratch,
        compiler_params=pltpu.CompilerParams(
            collective_id=0, has_side_effects=True, vmem_limit_bytes=52 * 2**20
        ),
        name="chebyshev",
    )(vectors, before, last, hamiltonian)
    if with_gram:
        return tuple(outs)
    (filtered,) = outs
    gathered = lax.all_gather(filtered, "vec", axis=1, tiled=True)
    partial_block = jnp.dot(
        filtered.T, gathered, precision=lax.Precision.HIGHEST, preferred_element_type=F32
    ) / (rows * n)
    return (filtered, lax.psum(partial_block, "domain"))


def solution(mesh):
    in_specs = (P("domain", "vec"), P("domain", None, None), P("domain", None), P("domain"))
    out_specs = (P("domain", "vec"), P("vec", None))
    return jax.shard_map(shards, mesh=mesh, in_specs=in_specs, out_specs=out_specs, check_vma=False)
```
